256 devices in a mesh: post: 64 (over x, z, core), rep: 4 (over y).
Axes of the slice: x: 4, y: 4, z: 8, core: 2. Of those that a mesh axis runs over, the one named last changes fastest.
Arguments:
- split_vectors: bfloat16 [2048, 192, 1024], P('post', None, 'rep'), may hold values from -6 to 6
- split_labels: int32 [2048, 192], P('post'), may hold values from 0 to 1, as said below
- split_lengths: int32 [2048], P('post'), may hold values from 144 to 192
- new_owners: int32 [2048, 2], P('post'), may hold values from 0 to 63, all different within a row; in each aligned block of 32 rows (0 to 31, 32 to 63, ...) at most 2 rows name the same one
- neighbour_ids: int32 [2048, 64], replicated, may hold values from 0 to 511, all different within a row
- resident_vectors: bfloat16 [512, 192, 1024], P('post', None, 'rep'), may hold values from -6 to 6
- resident_centroids: bfloat16 [512, 1024], P('post', 'rep'), may hold values from -1 to 1
- resident_lengths: int32 [512], P('post'), may hold values from 1 to 192
Outputs:
- new_postings: bfloat16 [4096, 2, 96, 1024], P('post', None, None, 'rep')
- new_centroids: float32 [2048, 2, 1024], P('post', None, 'rep')
- rescore: float32 [512, 192], P('post')
The draws below stay inside these ranges and needn't reach their ends.
Inputs may be any that keep to these rules, and one draw needn't show every extreme that they name: `split_labels`: rows at or past a posting's length carry label 1; each half of a split posting holds between 48 and 96 valid rows, and some split has both halves of exactly 96 rows. `new_owners`: the two halves of a split go to different owners; the halves of the splits of one index of post give at most 2 to any one owner. `neighbour_ids`: each split names 64 different postings.
All inputs are finite; a program needn't handle non-finite values.
Results may differ from the reference program's by a relative error of at most 0.0034.
Values may be sent and summed in bfloat16 or wider, within the bound.
No kernel may reach another device: no remote copies, remote signals or barrier semaphores. Data moves between devices by JAX's collectives and lax.ppermute only.
A program may use at most 128 MiB of HBM per device.

```python
import math
import jax
import jax.numpy as jnp
import numpy as np
from jax import lax

D = 1024
L = 192
NEIGH = 64
S_DEV = 32
HALF = 96
HSLOT = 2
SPLITS = 2048
RES = 512
N_POST = 64


def split_shared(key):
    base_key = jax.random.fold_in(key, 7)
    key_length, key_first, key_order = jax.random.split(base_key, 3)
    split_ids = jnp.arange(SPLITS)
    lengths = jax.random.randint(key_length, (SPLITS,), 3 * HALF // 2, L + 1)
    lengths = jnp.where(split_ids % 8 == 0, L, lengths)
    lowest = lengths - HALF
    first_count = lowest + jax.random.randint(key_first, (SPLITS,), 0, 1 << 20) % (HALF - lowest + 1)
    first_count = jnp.where(split_ids % 8 == 0, HALF, first_count)

    def shuffled(row_key):
        return jax.random.permutation(row_key, L)
    scores = jax.vmap(shuffled)(jax.random.split(key_order, SPLITS))
    row_ids = jnp.arange(L)
    scores = jnp.where(row_ids[None, :] < lengths[:, None], scores, L + row_ids[None, :])
    ranking = jnp.argsort(jnp.argsort(scores, axis=1, stable=True), axis=1, stable=True)
    labels = (ranking >= first_count[:, None]).astype(jnp.int32)
    return (lengths.astype(jnp.int32), labels)


def draw_split_lengths(key, part):
    return split_shared(key)[0]


def draw_split_labels(key, part):
    return split_shared(key)[1]


def place_ends(drawn, stream_key, least, high):
    shape = drawn.shape
    spot = [jax.random.randint(jax.random.fold_in(stream_key, axis), (), 0, shape[axis]) for axis in range(len(shape))]
    drawn = drawn.at[tuple(spot)].set(least)
    longest = shape.index(max(shape))
    spot[longest] = (spot[longest] + 1) % shape[longest]
    return drawn.at[tuple(spot)].set(high)


def steps_of(own_key, shape, cuts, smallest, top_value):
    gain = 1.0
    for axis_at, shards_of in cuts:
        draws = jax.random.uniform(jax.random.fold_in(jax.random.fold_in(own_key, 6), axis_at), (shards_of,), jnp.float32, smallest / len(cuts), top_value / len(cuts))
        gain = gain * jnp.repeat(jnp.exp(draws), shape[axis_at] // shards_of).reshape((-1,) + (1,) * (len(shape) - 1 - axis_at))
    return gain


def different_ones(rng, rows, amount, top, lift):
    order = jax.random.permutation(jax.random.fold_in(rng, 1), amount)
    favour = order
    for power in range(3):
        favour = favour * favour // amount
    favour = favour * lift // amount
    tickets = jax.random.randint(jax.random.fold_in(rng, 2), (rows, amount), 0, 4096) + favour
    fixed_rows = jax.random.permutation(jax.random.fold_in(rng, 3), rows)[jnp.arange(amount) % rows]
    tickets = jnp.where(jnp.arange(rows)[:, None] == fixed_rows[None, :], 1 << 14, tickets)
    merit = tickets * amount + jnp.arange(amount)
    return lax.top_k(merit.astype(jnp.int32), top)[1].astype(jnp.int32)


def assign_block(key, own, number, rows, amount, top, reach, lean):
    sequence = jax.random.permutation(key, amount)
    crowded, common = shares(amount, rows * top, reach, lean, True), shares(amount, rows * top, reach, lean, False)
    places = jnp.arange(amount)

    def named(sizes, turn):
        used = int((sizes > 0).sum())
        fixed = max(1, used // 4)
        shifted = fixed + (places - fixed + turn * (used - fixed)) % max(1, amount - fixed)
        return jnp.zeros((amount,), jnp.int32).at[sequence[jnp.where(places < fixed, places, shifted)]].set(jnp.asarray(sizes, jnp.int32))

    sizes = jnp.where(number % 4 == 0, named(crowded, number // 4), named(common, number - number // 4 - 1))
    mixed = jax.random.permutation(jax.random.fold_in(own, 3), amount)
    source_of, taker = mixed[0:amount // 2 * 2:2], mixed[1:amount // 2 * 2:2]
    margin = jnp.minimum(sizes[source_of] - 1, reach - sizes[taker]) // 2
    margin = jnp.where((source_of == sequence[0]) | (taker == sequence[0]) | (sizes[taker] == 0), 0, jnp.maximum(margin, 0))
    shifted = jax.random.randint(jax.random.fold_in(own, 4), (amount // 2,), 0, 1 << 20) % (margin + 1)
    sizes = sizes.at[source_of].add(-shifted).at[taker].add(shifted)
    items = jnp.searchsorted(jnp.cumsum(sizes), jnp.arange(rows * top), side="right").astype(jnp.int32)
    listing = items.reshape(top, rows).T
    listing = listing[jax.random.permutation(jax.random.fold_in(own, 1), rows)]
    turn = jax.random.randint(jax.random.fold_in(own, 2), (rows, 1), 0, top)
    return jnp.take_along_axis(listing, (jnp.arange(top)[None, :] + turn) % top, axis=1)


def shares(count, total, most, lean, full):
    portions = [(1 << 20) // math.isqrt(rank ** lean) + 1 for rank in range(1, count + 1)]
    largest = most if full else min(most, max(-(-total // count), total * portions[0] // sum(portions)))
    least = 1 if total - largest >= count - 1 else 0
    holding, rest = [largest] + [least] * (count - 1), total - largest - least * (count - 1)
    while rest > 0:
        free = [i for i in range(1, count) if holding[i] < largest] or [i for i in range(1, count) if holding[i] < most]
        mass, left = sum([portions[i] for i in free]), rest
        for i in free:
            addition = min(most - holding[i], max(1, left * portions[i] // mass), rest)
            holding[i] = holding[i] + addition
            rest = rest - addition
    return np.array(holding)


def gaussian(key, dims, spread, limit, cuts=(), kind=jnp.bfloat16):
    values = jax.random.normal(key, dims, jnp.float32) * spread
    if len(cuts) > 0:
        values = steps_of(key, dims, cuts, -0.22, 0.18) * values
    return jnp.clip(values, min=-limit, max=limit).astype(kind)


def setup_inputs(seed: int = 0) -> dict:
    streams_of = jax.random.split(jax.random.key(seed), 9)
    split_vectors = gaussian(streams_of[0], (SPLITS, L, D), 1.0, 6.0, ((0, 64), (2, 4)))
    split_labels = draw_split_labels(jax.random.fold_in(streams_of[8], 71), 0)
    split_lengths = draw_split_lengths(jax.random.fold_in(streams_of[8], 71), 0)
    new_owners_keys = jax.random.split(jax.random.fold_in(streams_of[3], 1), SPLITS // S_DEV)
    new_owners_turns = jax.random.permutation(jax.random.fold_in(streams_of[3], 3), SPLITS // S_DEV)
    new_owners = jax.vmap(lambda own, number: assign_block(jax.random.fold_in(streams_of[3], 2), own, number, S_DEV, N_POST, 2, HSLOT, 2))(new_owners_keys, new_owners_turns).reshape((SPLITS, 2))
    neighbour_ids = different_ones(streams_of[4], SPLITS, RES, NEIGH, 0)
    resident_vectors = gaussian(streams_of[5], (RES, L, D), 1.0, 6.0, ((0, 64), (2, 4)))
    resident_centroids = gaussian(streams_of[6], (RES, D), 0.15, 1.0, ((0, 64), (1, 4)))
    resident_lengths = place_ends(jax.random.randint(streams_of[7], (RES,), 1, L + 1), jax.random.fold_in(streams_of[7], 1), 1, L).astype(jnp.int32)
    return {"split_vectors": split_vectors, "split_labels": split_labels, "split_lengths": split_lengths, "new_owners": new_owners, "neighbour_ids": neighbour_ids, "resident_vectors": resident_vectors, "resident_centroids": resident_centroids, "resident_lengths": resident_lengths}


far_value = 1e+30

def pack_split(inputs):
    vectors, labels, length = inputs
    row_ids = jnp.arange(L)
    in_half = (row_ids[None, :] < length) & (labels[None, :] == jnp.arange(2)[:, None])
    member_int = in_half.astype(jnp.int32)
    half_rank = jnp.cumsum(member_int, axis=1) - member_int
    placement = in_half[:, None, :] & (half_rank[:, None, :] == jnp.arange(HALF)[None, :, None])
    packed = jnp.dot(placement.reshape(2 * HALF, L).astype(jnp.bfloat16), vectors, preferred_element_type=jnp.float32)
    packed = packed.astype(jnp.bfloat16).reshape(2, HALF, D)
    half_sums = jnp.dot(in_half.astype(jnp.bfloat16), vectors, preferred_element_type=jnp.float32)
    counts = lax.optimization_barrier(jnp.sum(member_int, axis=1)).astype(jnp.float32)
    return (packed, half_sums / counts[:, None])

def reference(split_vectors, split_labels, split_lengths, new_owners, neighbour_ids, resident_vectors, resident_centroids, resident_lengths):
    packed, new_centroids = lax.map(pack_split, (split_vectors, split_labels, split_lengths))
    owner_blocks = new_owners.reshape(N_POST, 2 * S_DEV).astype(jnp.int32)
    half_order = jnp.arange(2 * S_DEV)
    same_owner = (owner_blocks[:, :, None] == owner_blocks[:, None, :]) & (half_order[None, None, :] < half_order[None, :, None])
    slot_within = lax.optimization_barrier(jnp.sum(same_owner.astype(jnp.int32), axis=2)).astype(jnp.int32)
    source_ids = jnp.arange(N_POST, dtype=jnp.int32)[:, None]
    target_slot = ((owner_blocks * N_POST + source_ids) * HSLOT + slot_within).reshape(-1).astype(jnp.int32)
    stored = jnp.zeros((N_POST * N_POST * HSLOT, HALF, D), jnp.bfloat16)
    stored = stored.at[target_slot].set(packed.reshape(SPLITS * 2, HALF, D))
    new_postings = stored.reshape(N_POST * N_POST, HSLOT, HALF, D)
    centroid_b = new_centroids.astype(jnp.bfloat16).reshape(2 * SPLITS, D)
    centroid_wide = centroid_b.astype(jnp.float32)
    centroid_norm = lax.optimization_barrier(jnp.sum(centroid_wide * centroid_wide, axis=1))
    split_ids = jnp.broadcast_to(jnp.arange(SPLITS, dtype=jnp.int32)[:, None], (SPLITS, NEIGH))
    named = jnp.zeros((SPLITS, RES), jnp.int32).at[split_ids, neighbour_ids.astype(jnp.int32)].set(1)
    named = jnp.repeat(named, 2, axis=0).T

    def score_one(inputs):
        vectors, current, length, hit = inputs
        vector_wide = vectors.astype(jnp.float32)
        own_diff = vector_wide - current.astype(jnp.float32)[None, :]
        own = lax.optimization_barrier(jnp.sum(own_diff * own_diff, axis=1))
        row_norm = lax.optimization_barrier(jnp.sum(vector_wide * vector_wide, axis=1))
        cross = jnp.dot(vectors, centroid_b.T, preferred_element_type=jnp.float32)
        distance = row_norm[:, None] - 2.0 * cross + centroid_norm[None, :]
        distance = jnp.where(hit[None, :] > 0, distance, far_value)
        best_dist = jnp.minimum(own, lax.optimization_barrier(jnp.min(distance, axis=1)))
        score = (best_dist - row_norm) / math.sqrt(D)
        return jnp.where(jnp.arange(L) < length, score, 0.0)
    rescore = lax.map(score_one, (resident_vectors, resident_centroids, resident_lengths, named))
    return (new_postings, new_centroids, rescore)
```

```python
import math

import jax
import jax.numpy as jnp
from jax import lax
from jax.experimental import pallas as pl
from jax.experimental.pallas import tpu as pltpu
from jax.sharding import PartitionSpec as P

D = 1024
far_value = 1e30


def pack_kernel(owners_hbm, lengths_hbm, labels_hbm, vectors_hbm, out_ref, cents_ref, cents_b_ref,
                owners_ref, lengths_ref, lengths_vec, labels_ref, vectors_ref, rank_ref, packed_ref,
                zero_ref, sums_ref, slot_ref, count_ref, out_sem, small_sem, in_sem):
    n_rep = cents_b_ref.shape[0]
    s_local, length = labels_ref.shape
    half_rows = length // 2
    n_owner = count_ref.shape[0]
    group = 4
    n_group = s_local // group

    def fetch(g):
        rows = pl.ds(g * group, group)
        return pltpu.make_async_copy(vectors_hbm.at[rows], vectors_ref.at[rows], in_sem.at[g])

    small = [
        pltpu.make_async_copy(owners_hbm, owners_ref, small_sem.at[0]),
        pltpu.make_async_copy(lengths_hbm, lengths_ref, small_sem.at[1]),
        pltpu.make_async_copy(lengths_hbm, lengths_vec.at[0], small_sem.at[2]),
        pltpu.make_async_copy(labels_hbm, labels_ref, small_sem.at[3]),
    ]
    for copy in small:
        copy.start()
    for g in range(n_group):
        fetch(g).start()
    zero_ref[...] = jnp.zeros_like(zero_ref)
    for o in range(n_owner):
        count_ref[o] = 0
    for copy in small:
        copy.wait()

    @pl.loop(0, s_local // 4)
    def _(g):
        for j in range(4):
            for h in range(2):
                s = g * 4 + j
                owner = owners_ref[h, s]
                slot_ref[2 * s + h] = owner * 2 + count_ref[owner]
                count_ref[owner] = count_ref[owner] + 1

    before = (
        lax.broadcasted_iota(jnp.int32, (length, length), 0)
        < lax.broadcasted_iota(jnp.int32, (length, length), 1)
    )
    labels = labels_ref[...].astype(jnp.float32)
    rank_ref[...] = jnp.dot(
        labels.astype(jnp.bfloat16),
        before.astype(jnp.float32).astype(jnp.bfloat16),
        preferred_element_type=jnp.float32,
    )
    row_id = lax.broadcasted_iota(jnp.int32, (1, length), 1)
    place_id = lax.broadcasted_iota(jnp.int32, (length, length), 0)
    sum_id = lax.broadcasted_iota(jnp.int32, (16, length), 0)

    @pl.loop(0, n_group)
    def _(g):
        fetch(g).wait()
        sums = []
        for j in range(group):
            s = g * group + j
            label = labels_ref[pl.ds(s, 1), :]
            rank = rank_ref[pl.ds(s, 1), :].astype(jnp.int32)
            half = jnp.where(row_id < lengths_ref[s], label, 2)
            goes_to = jnp.where(
                half == 0, row_id - rank, jnp.where(half == 1, half_rows + rank, length)
            )
            placement = jnp.concatenate(
                [
                    jnp.where(goes_to == place_id, 1.0, 0.0).astype(jnp.bfloat16),
                    jnp.where(half == sum_id, 1.0, 0.0).astype(jnp.bfloat16),
                ],
                axis=0,
            )
            placed = jnp.dot(placement, vectors_ref[s], preferred_element_type=jnp.float32)
            packed_ref[2 * s] = placed[:half_rows].astype(jnp.bfloat16)
            packed_ref[2 * s + 1] = placed[half_rows:length].astype(jnp.bfloat16)
            for h in range(2):
                pltpu.make_async_copy(
                    packed_ref.at[2 * s + h], out_ref.at[slot_ref[2 * s + h]], out_sem
                ).start()
            sums.append(placed[length : length + 2])
        sums_ref[pl.ds(pl.multiple_of(g * 8, 8), 8), :] = jnp.concatenate(sums, axis=0)

        for j in range(n_owner // n_group):
            o = g * (n_owner // n_group) + j
            for k in range(2):
                @pl.when(count_ref[o] <= k)
                def _():
                    pltpu.make_async_copy(zero_ref, out_ref.at[o * 2 + k], out_sem).start()

    ones_total = jnp.sum(labels, axis=1, keepdims=True)
    same = lax.broadcasted_iota(jnp.int32, (s_local, s_local), 0) == lax.broadcasted_iota(
        jnp.int32, (s_local, s_local), 1
    )
    lengths = jnp.sum(
        jnp.where(same, lengths_vec[...].astype(jnp.float32), 0.0), axis=1, keepdims=True
    )
    first = length - ones_total
    which = lax.broadcasted_iota(jnp.int32, (2 * s_local, s_local), 0)
    split_id = lax.broadcasted_iota(jnp.int32, (2 * s_local, s_local), 1)
    counts = 0.0
    for h, count in enumerate((first, lengths - first)):
        pick = jnp.where(which == 2 * split_id + h, 1.0, 0.0).astype(jnp.bfloat16)
        wide = jnp.broadcast_to(count, (s_local, 128)).astype(jnp.bfloat16)
        counts += jnp.dot(pick, wide, preferred_element_type=jnp.float32)
    cents = sums_ref[...] / jnp.concatenate([counts] * (sums_ref.shape[1] // 128), axis=1)
    cents_ref[...] = cents
    sums_ref[...] = cents
    share = 2 * s_local // n_rep
    rep = lax.axis_index("rep")
    for k in range(n_rep):
        start = pl.multiple_of(lax.rem(rep + k, n_rep) * share, share)
        cents_b_ref[k] = sums_ref[pl.ds(start, share), :].astype(jnp.bfloat16)
    pltpu.make_async_copy(out_ref, out_ref, out_sem).wait()


def pack(split_vectors, split_labels, split_lengths, new_owners, n_post, n_rep):
    s_local, length, dims = split_vectors.shape
    half_rows = length // 2
    return pl.pallas_call(
        pack_kernel,
        out_shape=(
            jax.ShapeDtypeStruct((2 * n_post, half_rows, dims), jnp.bfloat16),
            jax.ShapeDtypeStruct((2 * s_local, dims), jnp.float32),
            jax.ShapeDtypeStruct((n_rep, 2 * s_local // n_rep, dims), jnp.bfloat16),
        ),
        in_specs=[pl.BlockSpec(memory_space=pltpu.HBM)] * 4,
        out_specs=(
            pl.BlockSpec(memory_space=pltpu.HBM),
            pl.BlockSpec(memory_space=pltpu.VMEM),
            pl.BlockSpec(memory_space=pltpu.VMEM),
        ),
        scratch_shapes=[
            pltpu.SMEM((2, s_local), jnp.int32),
            pltpu.SMEM((s_local,), jnp.int32),
            pltpu.VMEM((1, s_local), jnp.int32),
            pltpu.VMEM((s_local, length), jnp.int32),
            pltpu.VMEM((s_local, length, dims), jnp.bfloat16),
            pltpu.VMEM((s_local, length), jnp.float32),
            pltpu.VMEM((2 * s_local, half_rows, dims), jnp.bfloat16),
            pltpu.VMEM((half_rows, dims), jnp.bfloat16),
            pltpu.VMEM((2 * s_local, dims), jnp.float32),
            pltpu.SMEM((2 * s_local,), jnp.int32),
            pltpu.SMEM((n_post,), jnp.int32),
            pltpu.SemaphoreType.DMA,
            pltpu.SemaphoreType.DMA((4,)),
            pltpu.SemaphoreType.DMA((s_local // 4,)),
        ],
        compiler_params=pltpu.CompilerParams(vmem_limit_bytes=56 << 20),
        cost_estimate=pl.CostEstimate(flops=10**9, bytes_accessed=16 << 20, transcendentals=0),
        name="pack",
    )(new_owners.T, split_lengths, split_labels, split_vectors)


def score_kernel(r0, r1, r2, r3, cents_ref, hits_ref, out_ref):
    rows = (r0, r1, r2, r3)
    n_q, length, dims = r0.shape
    blocks = [cents_ref[:, k].reshape(-1, dims) for k in range(len(rows))]
    norm = 0.0
    for block in blocks:
        wide = block.astype(jnp.float32)
        norm += jnp.sum(wide * wide, axis=1, keepdims=True)
    for q in range(n_q):
        cross = 0.0
        for block, ref in zip(blocks, rows):
            cross += lax.dot_general(
                block, ref[q], (((1,), (1,)), ((), ())), preferred_element_type=jnp.float32
            )
        offset = jnp.where(hits_ref[:, q : q + 1] > 0, norm, far_value)
        out_ref[q : q + 1, :] = jnp.min(offset - 2.0 * cross, axis=0, keepdims=True)


def score(rows, cents, hits):
    n_q, length, dims = rows[0].shape
    return pl.pallas_call(
        score_kernel,
        out_shape=jax.ShapeDtypeStruct((n_q, length), jnp.float32),
        in_specs=[pl.BlockSpec(memory_space=pltpu.VMEM)] * 6,
        out_specs=pl.BlockSpec(memory_space=pltpu.VMEM),
        compiler_params=pltpu.CompilerParams(vmem_limit_bytes=40 << 20),
        cost_estimate=pl.CostEstimate(flops=4 * 10**9, bytes_accessed=6 << 20, transcendentals=0),
        name="score",
    )(*rows, cents, hits)


def shift(x, axis, k):
    n = lax.axis_size(axis)
    return lax.ppermute(x, axis, [(i, (i + k) % n) for i in range(n)])


def body(
    split_vectors,
    split_labels,
    split_lengths,
    new_owners,
    neighbour_ids,
    resident_vectors,
    resident_centroids,
    resident_lengths,
):
    n_post, n_rep = lax.axis_size("post"), lax.axis_size("rep")
    s_local, length, dim_share = split_vectors.shape
    res_local = resident_vectors.shape[0]
    outgoing, new_centroids, centroid_b = pack(
        split_vectors, split_labels, split_lengths, new_owners, n_post, n_rep
    )
    new_centroids = new_centroids.reshape(s_local, 2, dim_share)
    outgoing = outgoing.reshape(n_post, 2, length // 2, dim_share)
    new_postings = lax.all_to_all(outgoing, "post", split_axis=0, concat_axis=0, tiled=True)

    rows = [resident_vectors] + [shift(resident_vectors, "rep", k) for k in range(1, n_rep)]
    my_cents = jnp.stack(
        [centroid_b[0]] + [shift(centroid_b[k], "rep", k) for k in range(1, n_rep)]
    )
    cents = lax.all_gather(
        my_cents.reshape(-1, n_rep * dim_share), "post", axis=0, tiled=True
    ).reshape(n_post, n_rep, -1, dim_share)
    my_ids = lax.dynamic_index_in_dim(
        neighbour_ids.reshape(n_post, n_rep, s_local // n_rep, -1),
        lax.axis_index("rep"), 1, keepdims=False,
    ).reshape(n_post * s_local // n_rep, -1)
    my_postings = lax.axis_index("post") * res_local + jnp.arange(res_local)
    hits = jnp.any(my_ids[:, :, None] == my_postings[None, None, :], axis=1)
    hits = jnp.repeat(hits.astype(jnp.int32), 2, axis=0)
    best = score(rows, cents, hits)

    wide_cents = resident_centroids.astype(jnp.float32)[:, None, :]
    own = jnp.sum(wide_cents * (wide_cents - 2.0 * resident_vectors.astype(jnp.float32)), axis=2)
    both = jnp.stack([best, own])
    one, two, three = (shift(both, "rep", k) for k in (1, 2, 3))
    best_all = jnp.minimum(jnp.minimum(best, two[0]), jnp.minimum(one[0], three[0]))
    own_all = (own + two[1]) + (one[1] + three[1])
    scores = jnp.minimum(best_all, own_all) / math.sqrt(D)
    row_ids = jnp.arange(length)
    rescore = jnp.where(row_ids[None, :] < resident_lengths[:, None], scores, 0.0)
    return (new_postings, new_centroids, rescore)


def solution(mesh):
    return jax.shard_map(
        body,
        mesh=mesh,
        in_specs=(
            P("post", None, "rep"),
            P("post", None),
            P("post"),
            P("post", None),
            P(),
            P("post", None, "rep"),
            P("post", "rep"),
            P("post"),
        ),
        out_specs=(P("post", None, None, "rep"), P("post", None, "rep"), P("post", None)),
        check_vma=False,
    )
```

```python
import functools
import math

import jax
import jax.numpy as jnp
from jax import lax
from jax.experimental import pallas as pl
from jax.experimental.pallas import tpu as pltpu
from jax.sharding import PartitionSpec as P

D = 1024
far_value = 1e30
N_X, N_Z, N_CORE = 4, 8, 2


def centroid_kernel(lengths_hbm, labels_hbm, vectors_hbm, cents_ref, copies_ref,
                    lengths_vec, labels_ref, vectors_ref, sums_ref, half_ref, small_sem, in_sem):
    s_local, length = labels_ref.shape
    group = 4
    n_group = s_local // group

    def fetch(g):
        rows = pl.ds(g * group, group)
        return pltpu.make_async_copy(vectors_hbm.at[rows], vectors_ref.at[rows], in_sem.at[g])

    small = [
        pltpu.make_async_copy(lengths_hbm, lengths_vec.at[0], small_sem.at[0]),
        pltpu.make_async_copy(labels_hbm, labels_ref, small_sem.at[1]),
    ]
    for copy in small:
        copy.start()
    for g in range(n_group):
        fetch(g).start()
    for copy in small:
        copy.wait()

    same = lax.broadcasted_iota(jnp.int32, (s_local, s_local), 0) == lax.broadcasted_iota(
        jnp.int32, (s_local, s_local), 1
    )
    lengths = jnp.sum(
        jnp.where(same, lengths_vec[...].astype(jnp.float32), 0.0), axis=1, keepdims=True
    )
    row_id = lax.broadcasted_iota(jnp.int32, (s_local, length), 1).astype(jnp.float32)
    half_ref[...] = jnp.where(row_id < lengths, labels_ref[...], 2)
    sum_id = lax.broadcasted_iota(jnp.int32, (16, length), 0)
    for g in range(n_group):
        fetch(g).wait()
        sums = []
        for s in range(g * group, (g + 1) * group):
            member = jnp.where(half_ref[s : s + 1, :] == sum_id, 1.0, 0.0).astype(jnp.bfloat16)
            sums.append(
                jnp.dot(member, vectors_ref[s], preferred_element_type=jnp.float32)[:2]
            )
        sums_ref[g * 8 : g * 8 + 8, :] = jnp.concatenate(sums, axis=0)

    which = lax.broadcasted_iota(jnp.int32, (2 * s_local, s_local), 0)
    split_id = lax.broadcasted_iota(jnp.int32, (2 * s_local, s_local), 1)
    counts = 0.0
    for h in range(2):
        count = jnp.sum(jnp.where(half_ref[...] == h, 1.0, 0.0), axis=1, keepdims=True)
        pick = jnp.where(which == 2 * split_id + h, 1.0, 0.0).astype(jnp.bfloat16)
        wide = jnp.broadcast_to(count, (s_local, 128)).astype(jnp.bfloat16)
        counts += jnp.dot(pick, wide, preferred_element_type=jnp.float32)
    cents = sums_ref[...] / jnp.concatenate([counts] * (sums_ref.shape[1] // 128), axis=1)
    cents_ref[...] = cents
    rounded = cents.astype(jnp.bfloat16)
    for i in range(copies_ref.shape[0]):
        copies_ref[i] = rounded


def centroids(split_vectors, split_labels, split_lengths):
    s_local, length, dims = split_vectors.shape
    return pl.pallas_call(
        centroid_kernel,
        out_shape=(
            jax.ShapeDtypeStruct((2 * s_local, dims), jnp.float32),
            jax.ShapeDtypeStruct((N_Z, 2 * s_local, dims), jnp.bfloat16),
        ),
        in_specs=[pl.BlockSpec(memory_space=pltpu.HBM)] * 3,
        out_specs=(pl.BlockSpec(memory_space=pltpu.VMEM),) * 2,
        scratch_shapes=[
            pltpu.VMEM((1, s_local), jnp.int32),
            pltpu.VMEM((s_local, length), jnp.int32),
            pltpu.VMEM((s_local, length, dims), jnp.bfloat16),
            pltpu.VMEM((2 * s_local, dims), jnp.float32),
            pltpu.VMEM((s_local, length), jnp.int32),
            pltpu.SemaphoreType.DMA((2,)),
            pltpu.SemaphoreType.DMA((s_local // 4,)),
        ],
        compiler_params=pltpu.CompilerParams(vmem_limit_bytes=56 << 20),
        cost_estimate=pl.CostEstimate(flops=10**8, bytes_accessed=4 << 20, transcendentals=0),
        name="centroids",
    )(split_lengths, split_labels, split_vectors)


def pack_kernel(owners_hbm, lengths_hbm, labels_hbm, vectors_hbm, out_ref,
                owners_ref, lengths_ref, labels_ref, vectors_ref, rank_ref, packed_ref,
                zero_ref, slot_ref, count_ref, out_sem, small_sem, in_sem):
    s_local, length = labels_ref.shape
    half_rows = length // 2
    n_owner = count_ref.shape[0]
    group = 4
    n_group = s_local // group

    def fetch(g):
        rows = pl.ds(g * group, group)
        return pltpu.make_async_copy(vectors_hbm.at[rows], vectors_ref.at[rows], in_sem.at[g])

    small = [
        pltpu.make_async_copy(owners_hbm, owners_ref, small_sem.at[0]),
        pltpu.make_async_copy(lengths_hbm, lengths_ref, small_sem.at[1]),
        pltpu.make_async_copy(labels_hbm, labels_ref, small_sem.at[2]),
    ]
    for copy in small:
        copy.start()
    for g in range(n_group):
        fetch(g).start()
    zero_ref[...] = jnp.zeros_like(zero_ref)
    for o in range(n_owner):
        count_ref[o] = 0
    for copy in small:
        copy.wait()

    @pl.loop(0, s_local // 4)
    def _(g):
        for j in range(4):
            for h in range(2):
                s = g * 4 + j
                owner = owners_ref[h, s]
                slot_ref[2 * s + h] = owner * 2 + count_ref[owner]
                count_ref[owner] = count_ref[owner] + 1

    before = (
        lax.broadcasted_iota(jnp.int32, (length, length), 0)
        < lax.broadcasted_iota(jnp.int32, (length, length), 1)
    )
    labels = labels_ref[...].astype(jnp.float32)
    rank_ref[...] = jnp.dot(
        labels.astype(jnp.bfloat16),
        before.astype(jnp.float32).astype(jnp.bfloat16),
        preferred_element_type=jnp.float32,
    )
    row_id = lax.broadcasted_iota(jnp.int32, (1, length), 1)
    place_id = lax.broadcasted_iota(jnp.int32, (length, length), 0)

    @pl.loop(0, n_group)
    def _(g):
        fetch(g).wait()
        for j in range(group):
            s = g * group + j
            label = labels_ref[pl.ds(s, 1), :]
            rank = rank_ref[pl.ds(s, 1), :].astype(jnp.int32)
            half = jnp.where(row_id < lengths_ref[s], label, 2)
            goes_to = jnp.where(
                half == 0, row_id - rank, jnp.where(half == 1, half_rows + rank, length)
            )
            placement = jnp.where(goes_to == place_id, 1.0, 0.0).astype(jnp.bfloat16)
            placed = jnp.dot(placement, vectors_ref[s], preferred_element_type=jnp.float32)
            packed_ref[2 * s] = placed[:half_rows].astype(jnp.bfloat16)
            packed_ref[2 * s + 1] = placed[half_rows:length].astype(jnp.bfloat16)
            for h in range(2):
                pltpu.make_async_copy(
                    packed_ref.at[2 * s + h], out_ref.at[slot_ref[2 * s + h]], out_sem
                ).start()

        for j in range(n_owner // n_group):
            o = g * (n_owner // n_group) + j
            for k in range(2):
                @pl.when(count_ref[o] <= k)
                def _():
                    pltpu.make_async_copy(zero_ref, out_ref.at[o * 2 + k], out_sem).start()

    pltpu.make_async_copy(out_ref, out_ref, out_sem).wait()


def pack(split_vectors, split_labels, split_lengths, new_owners, n_post):
    s_local, length, dims = split_vectors.shape
    half_rows = length // 2
    return pl.pallas_call(
        pack_kernel,
        out_shape=jax.ShapeDtypeStruct((2 * n_post, half_rows, dims), jnp.bfloat16),
        in_specs=[pl.BlockSpec(memory_space=pltpu.HBM)] * 4,
        out_specs=pl.BlockSpec(memory_space=pltpu.HBM),
        scratch_shapes=[
            pltpu.SMEM((2, s_local), jnp.int32),
            pltpu.SMEM((s_local,), jnp.int32),
            pltpu.VMEM((s_local, length), jnp.int32),
            pltpu.VMEM((s_local, length, dims), jnp.bfloat16),
            pltpu.VMEM((s_local, length), jnp.float32),
            pltpu.VMEM((2 * s_local, half_rows, dims), jnp.bfloat16),
            pltpu.VMEM((half_rows, dims), jnp.bfloat16),
            pltpu.SMEM((2 * s_local,), jnp.int32),
            pltpu.SMEM((n_post,), jnp.int32),
            pltpu.SemaphoreType.DMA,
            pltpu.SemaphoreType.DMA((3,)),
            pltpu.SemaphoreType.DMA((s_local // 4,)),
        ],
        compiler_params=pltpu.CompilerParams(vmem_limit_bytes=56 << 20),
        cost_estimate=pl.CostEstimate(flops=10**9, bytes_accessed=16 << 20, transcendentals=0),
        name="pack",
    )(new_owners.T, split_lengths, split_labels, split_vectors)


def score_kernel(*refs):
    n_rows = len(refs) - N_X * N_CORE - 2
    rows, pieces = refs[:n_rows], refs[n_rows:-2]
    hits_ref, out_ref = refs[-2:]
    n_q = rows[0].shape[0]
    blocks = [jnp.concatenate([p[k] for p in pieces], axis=0) for k in range(n_rows)]
    norm = 0.0
    for block in blocks:
        wide = block.astype(jnp.float32)
        norm += jnp.sum(wide * wide, axis=1, keepdims=True)
    for q in range(n_q):
        cross = 0.0
        for block, ref in zip(blocks, rows):
            cross += lax.dot_general(
                block, ref[q], (((1,), (1,)), ((), ())), preferred_element_type=jnp.float32
            )
        offset = jnp.where(hits_ref[:, q : q + 1] > 0, norm, far_value)
        out_ref[q : q + 1, :] = jnp.min(offset - 2.0 * cross, axis=0, keepdims=True)


def score(rows, pieces, hits):
    n_q, length, dims = rows[0].shape
    return pl.pallas_call(
        score_kernel,
        out_shape=jax.ShapeDtypeStruct((n_q, length), jnp.float32),
        in_specs=[pl.BlockSpec(memory_space=pltpu.VMEM)] * (len(rows) + len(pieces) + 1),
        out_specs=pl.BlockSpec(memory_space=pltpu.VMEM),
        compiler_params=pltpu.CompilerParams(vmem_limit_bytes=40 << 20),
        cost_estimate=pl.CostEstimate(flops=4 * 10**9, bytes_accessed=6 << 20, transcendentals=0),
        name="score",
    )(*rows, *pieces, hits)


def store_kernel(got, out, held, in_sems, out_sems):
    n_copies = in_sems.shape[0]
    step = got.shape[0] // n_copies
    rows = [pl.ds(i * step, step) for i in range(n_copies)]
    reads = [
        pltpu.make_async_copy(got.at[r], held.at[r], in_sems.at[i]) for i, r in enumerate(rows)
    ]
    writes = [
        pltpu.make_async_copy(held.at[r], out.at[r], out_sems.at[i]) for i, r in enumerate(rows)
    ]
    for read in reads:
        read.start()
    for read, write in zip(reads, writes):
        read.wait()
        write.start()
    for write in writes:
        write.wait()


def store(got):
    n_copies = 16
    return pl.pallas_call(
        store_kernel,
        out_shape=jax.ShapeDtypeStruct(got.shape, got.dtype),
        in_specs=[pl.BlockSpec(memory_space=pltpu.HBM)],
        out_specs=pl.BlockSpec(memory_space=pltpu.HBM),
        scratch_shapes=[
            pltpu.VMEM(got.shape, got.dtype),
            pltpu.SemaphoreType.DMA((n_copies,)),
            pltpu.SemaphoreType.DMA((n_copies,)),
        ],
        compiler_params=pltpu.CompilerParams(vmem_limit_bytes=56 << 20),
        cost_estimate=pl.CostEstimate(flops=0, bytes_accessed=12 << 20, transcendentals=0),
        name="store",
    )(got)


def shift(x, axis, k):
    n = lax.axis_size(axis)
    return lax.ppermute(x, axis, [(i, (i + k) % n) for i in range(n)])


def shift_in_plane(x, by_x, by_core):
    pairs = []
    for i in range(N_X * N_Z * N_CORE):
        at_x, at_z, core = i // (N_Z * N_CORE), i // N_CORE % N_Z, i % N_CORE
        to = ((at_x + by_x) % N_X * N_Z + at_z) * N_CORE + (core + by_core) % N_CORE
        pairs.append((i, to))
    return lax.ppermute(x, "post", pairs)


def body(
    split_vectors,
    split_labels,
    split_lengths,
    new_owners,
    neighbour_ids,
    resident_vectors,
    resident_centroids,
    resident_lengths,
):
    n_post, n_rep = lax.axis_size("post"), lax.axis_size("rep")
    s_local, length, dim_share = split_vectors.shape
    res_local = resident_vectors.shape[0]
    new_centroids, copies = centroids(split_vectors, split_labels, split_lengths)

    z_groups = [
        [(x * N_Z + z) * N_CORE + core for z in range(N_Z)]
        for x in range(N_X) for core in range(N_CORE)
    ]
    on_z = lax.all_to_all(
        copies, "post", split_axis=0, concat_axis=0, tiled=True, axis_index_groups=z_groups
    )
    new_centroids, split_vectors = lax.optimization_barrier((new_centroids, split_vectors))
    outgoing = pack(split_vectors, split_labels, split_lengths, new_owners, n_post)
    on_z, outgoing, resident_vectors, resident_centroids, neighbour_ids = lax.optimization_barrier(
        (on_z, outgoing, resident_vectors, resident_centroids, neighbour_ids)
    )
    outgoing = outgoing.reshape(n_post, 2, length // 2, dim_share)
    new_postings = store(
        lax.all_to_all(outgoing, "post", split_axis=0, concat_axis=0, tiled=True)
    )
    new_centroids = new_centroids.reshape(s_local, 2, dim_share)

    rep, post = lax.axis_index("rep"), lax.axis_index("post")
    per_rep = N_Z // n_rep
    parts = [
        lax.dynamic_slice_in_dim(on_z, lax.rem(rep + k, n_rep) * per_rep, per_rep).reshape(
            per_rep * 2 * s_local, dim_share
        )
        for k in range(n_rep)
    ]
    mine = jnp.stack([parts[0]] + [shift(parts[k], "rep", k) for k in range(1, n_rep)])
    pieces = [mine] + [shift_in_plane(mine, k, 0) for k in (1, 3, 2)]
    pieces += [shift_in_plane(piece, 0, 1) for piece in pieces]
    rows = [resident_vectors] + [shift(resident_vectors, "rep", k) for k in range(1, n_rep)]

    my_postings = post * res_local + jnp.arange(res_local)
    ids = []
    for by_core in (0, 1):
        for by_x in (0, 1, 3, 2):
            from_x = lax.rem(post // (N_Z * N_CORE) + N_X - by_x, N_X)
            from_core = lax.rem(post + by_core, N_CORE)
            for z in range(per_rep):
                source = (from_x * N_Z + rep * per_rep + z) * N_CORE + from_core
                ids.append(lax.dynamic_slice_in_dim(neighbour_ids, source * s_local, s_local))
    hits = jnp.any(jnp.concatenate(ids)[:, :, None] == my_postings[None, None, :], axis=1)
    hits = jnp.repeat(hits.astype(jnp.int32), 2, axis=0)
    wide_cents = resident_centroids.astype(jnp.float32)[:, None, :]
    own = jnp.sum(wide_cents * (wide_cents - 2.0 * resident_vectors.astype(jnp.float32)), axis=2)
    best = score(rows, pieces, hits)
    both = jnp.stack([best, own])
    one, two, three = (shift(both, "rep", k) for k in (1, 2, 3))
    best_all = jnp.minimum(jnp.minimum(best, two[0]), jnp.minimum(one[0], three[0]))
    own_all = (own + two[1]) + (one[1] + three[1])
    scores = jnp.minimum(best_all, own_all) / math.sqrt(D)
    row_ids = jnp.arange(length)
    rescore = jnp.where(row_ids[None, :] < resident_lengths[:, None], scores, 0.0)
    return (new_postings, new_centroids, rescore)


def solution(mesh):
    return jax.shard_map(
        body,
        mesh=mesh,
        in_specs=(
            P("post", None, "rep"),
            P("post", None),
            P("post"),
            P("post", None),
            P(),
            P("post", None, "rep"),
            P("post", "rep"),
            P("post"),
        ),
        out_specs=(P("post", None, None, "rep"), P("post", None, "rep"), P("post", None)),
        check_vma=False,
    )
```

```python
import functools
import math

import jax
import jax.numpy as jnp
from jax import lax
from jax.experimental import pallas as pl
from jax.experimental.pallas import tpu as pltpu
from jax.sharding import PartitionSpec as P

D = 1024
far_value = 1e30
N_X, N_Z, N_CORE = 4, 8, 2


def centroid_kernel(lengths_hbm, labels_hbm, vectors_hbm, cents_ref, copies_ref,
                    lengths_vec, labels_ref, vectors_ref, sums_ref, half_ref, small_sem, in_sem):
    s_local, length = labels_ref.shape
    group = 8
    n_group = s_local // group

    def fetch(g):
        rows = pl.ds(g * group, group)
        return pltpu.make_async_copy(vectors_hbm.at[rows], vectors_ref.at[rows], in_sem.at[g])

    small = [
        pltpu.make_async_copy(lengths_hbm, lengths_vec.at[0], small_sem.at[0]),
        pltpu.make_async_copy(labels_hbm, labels_ref, small_sem.at[1]),
    ]
    for copy in small:
        copy.start()
    for g in range(n_group):
        fetch(g).start()
    for copy in small:
        copy.wait()

    same = lax.broadcasted_iota(jnp.int32, (s_local, s_local), 0) == lax.broadcasted_iota(
        jnp.int32, (s_local, s_local), 1
    )
    lengths = jnp.sum(
        jnp.where(same, lengths_vec[...].astype(jnp.float32), 0.0), axis=1, keepdims=True
    )
    row_id = lax.broadcasted_iota(jnp.int32, (s_local, length), 1).astype(jnp.float32)
    half_ref[...] = jnp.where(row_id < lengths, labels_ref[...], -100)
    sum_id = lax.broadcasted_iota(jnp.int32, (16, length), 0)
    for g in range(n_group):
        fetch(g).wait()
        total = 0.0
        for j in range(group):
            s = g * group + j
            member = jnp.where(half_ref[s : s + 1, :] + 2 * j == sum_id, 1.0, 0.0)
            total += jnp.dot(
                member.astype(jnp.bfloat16), vectors_ref[s], preferred_element_type=jnp.float32
            )
        sums_ref[g * 2 * group : (g + 1) * 2 * group, :] = total[: 2 * group]

    which = lax.broadcasted_iota(jnp.int32, (2 * s_local, s_local), 0)
    split_id = lax.broadcasted_iota(jnp.int32, (2 * s_local, s_local), 1)
    counts = 0.0
    for h in range(2):
        count = jnp.sum(jnp.where(half_ref[...] == h, 1.0, 0.0), axis=1, keepdims=True)
        pick = jnp.where(which == 2 * split_id + h, 1.0, 0.0).astype(jnp.bfloat16)
        wide = jnp.broadcast_to(count, (s_local, 128)).astype(jnp.bfloat16)
        counts += jnp.dot(pick, wide, preferred_element_type=jnp.float32)
    cents = sums_ref[...] / jnp.concatenate([counts] * (sums_ref.shape[1] // 128), axis=1)
    cents_ref[...] = cents
    rounded = cents.astype(jnp.bfloat16)
    for i in range(copies_ref.shape[0]):
        copies_ref[i] = rounded


def centroids(split_vectors, split_labels, split_lengths):
    s_local, length, dims = split_vectors.shape
    return pl.pallas_call(
        centroid_kernel,
        out_shape=(
            jax.ShapeDtypeStruct((2 * s_local, dims), jnp.float32),
            jax.ShapeDtypeStruct((N_Z, 2 * s_local, dims), jnp.bfloat16),
        ),
        in_specs=[pl.BlockSpec(memory_space=pltpu.HBM)] * 3,
        out_specs=(pl.BlockSpec(memory_space=pltpu.VMEM),) * 2,
        scratch_shapes=[
            pltpu.VMEM((1, s_local), jnp.int32),
            pltpu.VMEM((s_local, length), jnp.int32),
            pltpu.VMEM((s_local, length, dims), jnp.bfloat16),
            pltpu.VMEM((2 * s_local, dims), jnp.float32),
            pltpu.VMEM((s_local, length), jnp.int32),
            pltpu.SemaphoreType.DMA((2,)),
            pltpu.SemaphoreType.DMA((s_local // 8,)),
        ],
        compiler_params=pltpu.CompilerParams(vmem_limit_bytes=56 << 20),
        cost_estimate=pl.CostEstimate(flops=10**8, bytes_accessed=4 << 20, transcendentals=0),
        name="centroids",
    )(split_lengths, split_labels, split_vectors)


def pack_kernel(owners_hbm, lengths_hbm, labels_hbm, vectors_hbm, out_ref,
                owners_ref, lengths_ref, labels_ref, vectors_ref, rank_ref, packed_ref,
                zero_ref, slot_ref, count_ref, out_sem, small_sem, in_sem):
    s_local, length = labels_ref.shape
    half_rows = length // 2
    n_owner = count_ref.shape[0]
    group = 4
    n_group = s_local // group

    def fetch(g):
        rows = pl.ds(g * group, group)
        return pltpu.make_async_copy(vectors_hbm.at[rows], vectors_ref.at[rows], in_sem.at[g])

    small = [
        pltpu.make_async_copy(owners_hbm, owners_ref, small_sem.at[0]),
        pltpu.make_async_copy(lengths_hbm, lengths_ref, small_sem.at[1]),
        pltpu.make_async_copy(labels_hbm, labels_ref, small_sem.at[2]),
    ]
    for copy in small:
        copy.start()
    for g in range(n_group):
        fetch(g).start()
    zero_ref[...] = jnp.zeros_like(zero_ref)
    for o in range(n_owner):
        count_ref[o] = 0
    for copy in small:
        copy.wait()

    @pl.loop(0, s_local // 4)
    def _(g):
        for j in range(4):
            for h in range(2):
                s = g * 4 + j
                owner = owners_ref[h, s]
                slot_ref[2 * s + h] = owner * 2 + count_ref[owner]
                count_ref[owner] = count_ref[owner] + 1

    before = (
        lax.broadcasted_iota(jnp.int32, (length, length), 0)
        < lax.broadcasted_iota(jnp.int32, (length, length), 1)
    )
    labels = labels_ref[...].astype(jnp.float32)
    rank_ref[...] = jnp.dot(
        labels.astype(jnp.bfloat16),
        before.astype(jnp.float32).astype(jnp.bfloat16),
        preferred_element_type=jnp.float32,
    )
    row_id = lax.broadcasted_iota(jnp.int32, (1, length), 1)
    place_id = lax.broadcasted_iota(jnp.int32, (length, length), 0)

    @pl.loop(0, n_group)
    def _(g):
        fetch(g).wait()
        for j in range(group):
            s = g * group + j
            label = labels_ref[pl.ds(s, 1), :]
            rank = rank_ref[pl.ds(s, 1), :].astype(jnp.int32)
            half = jnp.where(row_id < lengths_ref[s], label, 2)
            goes_to = jnp.where(
                half == 0, row_id - rank, jnp.where(half == 1, half_rows + rank, length)
            )
            placement = jnp.where(goes_to == place_id, 1.0, 0.0).astype(jnp.bfloat16)
            placed = jnp.dot(placement, vectors_ref[s], preferred_element_type=jnp.float32)
            packed_ref[2 * s] = placed[:half_rows].astype(jnp.bfloat16)
            packed_ref[2 * s + 1] = placed[half_rows:length].astype(jnp.bfloat16)
            for h in range(2):
                pltpu.make_async_copy(
                    packed_ref.at[2 * s + h], out_ref.at[slot_ref[2 * s + h]], out_sem
                ).start()

        for j in range(n_owner // n_group):
            o = g * (n_owner // n_group) + j
            for k in range(2):
                @pl.when(count_ref[o] <= k)
                def _():
                    pltpu.make_async_copy(zero_ref, out_ref.at[o * 2 + k], out_sem).start()

    pltpu.make_async_copy(out_ref, out_ref, out_sem).wait()


def pack(split_vectors, split_labels, split_lengths, new_owners, n_post):
    s_local, length, dims = split_vectors.shape
    half_rows = length // 2
    return pl.pallas_call(
        pack_kernel,
        out_shape=jax.ShapeDtypeStruct((2 * n_post, half_rows, dims), jnp.bfloat16),
        in_specs=[pl.BlockSpec(memory_space=pltpu.HBM)] * 4,
        out_specs=pl.BlockSpec(memory_space=pltpu.HBM),
        scratch_shapes=[
            pltpu.SMEM((2, s_local), jnp.int32),
            pltpu.SMEM((s_local,), jnp.int32),
            pltpu.VMEM((s_local, length), jnp.int32),
            pltpu.VMEM((s_local, length, dims), jnp.bfloat16),
            pltpu.VMEM((s_local, length), jnp.float32),
            pltpu.VMEM((2 * s_local, half_rows, dims), jnp.bfloat16),
            pltpu.VMEM((half_rows, dims), jnp.bfloat16),
            pltpu.SMEM((2 * s_local,), jnp.int32),
            pltpu.SMEM((n_post,), jnp.int32),
            pltpu.SemaphoreType.DMA,
            pltpu.SemaphoreType.DMA((3,)),
            pltpu.SemaphoreType.DMA((s_local // 4,)),
        ],
        compiler_params=pltpu.CompilerParams(vmem_limit_bytes=56 << 20),
        cost_estimate=pl.CostEstimate(flops=10**9, bytes_accessed=16 << 20, transcendentals=0),
        name="pack",
    )(new_owners.T, split_lengths, split_labels, split_vectors)


def score_kernel(*refs):
    n_rows = len(refs) - N_X * N_CORE - 2
    rows, pieces = refs[:n_rows], refs[n_rows:-2]
    hits_ref, out_ref = refs[-2:]
    n_q = rows[0].shape[0]
    blocks = [jnp.concatenate([p[k] for p in pieces], axis=0) for k in range(n_rows)]
    norm = 0.0
    for block in blocks:
        wide = block.astype(jnp.float32)
        norm += jnp.sum(wide * wide, axis=1, keepdims=True)
    for q in range(n_q):
        cross = 0.0
        for block, ref in zip(blocks, rows):
            cross += lax.dot_general(
                block, ref[q], (((1,), (1,)), ((), ())), preferred_element_type=jnp.float32
            )
        offset = jnp.where(hits_ref[:, q : q + 1] > 0, norm, far_value)
        out_ref[q : q + 1, :] = jnp.min(offset - 2.0 * cross, axis=0, keepdims=True)


def score(rows, pieces, hits):
    n_q, length, dims = rows[0].shape
    return pl.pallas_call(
        score_kernel,
        out_shape=jax.ShapeDtypeStruct((n_q, length), jnp.float32),
        in_specs=[pl.BlockSpec(memory_space=pltpu.VMEM)] * (len(rows) + len(pieces) + 1),
        out_specs=pl.BlockSpec(memory_space=pltpu.VMEM),
        compiler_params=pltpu.CompilerParams(vmem_limit_bytes=40 << 20),
        cost_estimate=pl.CostEstimate(flops=4 * 10**9, bytes_accessed=6 << 20, transcendentals=0),
        name="score",
    )(*rows, *pieces, hits)


def store_kernel(got, out, held, in_sems, out_sems):
    n_copies = in_sems.shape[0]
    step = got.shape[0] // n_copies
    rows = [pl.ds(i * step, step) for i in range(n_copies)]
    reads = [
        pltpu.make_async_copy(got.at[r], held.at[r], in_sems.at[i]) for i, r in enumerate(rows)
    ]
    writes = [
        pltpu.make_async_copy(held.at[r], out.at[r], out_sems.at[i]) for i, r in enumerate(rows)
    ]
    for read in reads:
        read.start()
    for read, write in zip(reads, writes):
        read.wait()
        write.start()
    for write in writes:
        write.wait()


def store(got):
    n_copies = 4
    return pl.pallas_call(
        store_kernel,
        out_shape=jax.ShapeDtypeStruct(got.shape, got.dtype),
        in_specs=[pl.BlockSpec(memory_space=pltpu.HBM)],
        out_specs=pl.BlockSpec(memory_space=pltpu.HBM),
        scratch_shapes=[
            pltpu.VMEM(got.shape, got.dtype),
            pltpu.SemaphoreType.DMA((n_copies,)),
            pltpu.SemaphoreType.DMA((n_copies,)),
        ],
        compiler_params=pltpu.CompilerParams(vmem_limit_bytes=56 << 20),
        cost_estimate=pl.CostEstimate(flops=0, bytes_accessed=12 << 20, transcendentals=0),
        name="store",
    )(got)


def shift(x, axis, k):
    n = lax.axis_size(axis)
    return lax.ppermute(x, axis, [(i, (i + k) % n) for i in range(n)])


def shift_in_plane(x, by_x, by_core):
    pairs = []
    for i in range(N_X * N_Z * N_CORE):
        at_x, at_z, core = i // (N_Z * N_CORE), i // N_CORE % N_Z, i % N_CORE
        to = ((at_x + by_x) % N_X * N_Z + at_z) * N_CORE + (core + by_core) % N_CORE
        pairs.append((i, to))
    return lax.ppermute(x, "post", pairs)


def body(
    split_vectors,
    split_labels,
    split_lengths,
    new_owners,
    neighbour_ids,
    resident_vectors,
    resident_centroids,
    resident_lengths,
):
    n_post, n_rep = lax.axis_size("post"), lax.axis_size("rep")
    s_local, length, dim_share = split_vectors.shape
    res_local = resident_vectors.shape[0]
    new_centroids, copies = centroids(split_vectors, split_labels, split_lengths)

    z_groups = [
        [(x * N_Z + z) * N_CORE + core for z in range(N_Z)]
        for x in range(N_X) for core in range(N_CORE)
    ]
    on_z = lax.all_to_all(
        copies, "post", split_axis=0, concat_axis=0, tiled=True, axis_index_groups=z_groups
    )
    new_centroids, split_vectors = lax.optimization_barrier((new_centroids, split_vectors))
    outgoing = pack(split_vectors, split_labels, split_lengths, new_owners, n_post)
    on_z, outgoing, resident_vectors, resident_centroids, neighbour_ids = lax.optimization_barrier(
        (on_z, outgoing, resident_vectors, resident_centroids, neighbour_ids)
    )
    outgoing = outgoing.reshape(n_post, 2, length // 2, dim_share)
    new_postings = store(
        lax.all_to_all(outgoing, "post", split_axis=0, concat_axis=0, tiled=True)
    )
    new_centroids = new_centroids.reshape(s_local, 2, dim_share)

    rep, post = lax.axis_index("rep"), lax.axis_index("post")
    per_rep = N_Z // n_rep
    parts = [
        lax.dynamic_slice_in_dim(on_z, lax.rem(rep + k, n_rep) * per_rep, per_rep).reshape(
            per_rep * 2 * s_local, dim_share
        )
        for k in range(n_rep)
    ]
    mine = jnp.stack([parts[0]] + [shift(parts[k], "rep", k) for k in range(1, n_rep)])
    pieces = [mine] + [shift_in_plane(mine, k, 0) for k in (1, 3, 2)]
    pieces += [shift_in_plane(piece, 0, 1) for piece in pieces]
    rows = [resident_vectors] + [shift(resident_vectors, "rep", k) for k in range(1, n_rep)]

    my_postings = post * res_local + jnp.arange(res_local)
    ids = []
    for by_core in (0, 1):
        for by_x in (0, 1, 3, 2):
            from_x = lax.rem(post // (N_Z * N_CORE) + N_X - by_x, N_X)
            from_core = lax.rem(post + by_core, N_CORE)
            for z in range(per_rep):
                source = (from_x * N_Z + rep * per_rep + z) * N_CORE + from_core
                ids.append(lax.dynamic_slice_in_dim(neighbour_ids, source * s_local, s_local))
    hits = jnp.any(jnp.concatenate(ids)[:, :, None] == my_postings[None, None, :], axis=1)
    hits = jnp.repeat(hits.astype(jnp.int32), 2, axis=0)
    wide_cents = resident_centroids.astype(jnp.float32)[:, None, :]
    own = jnp.sum(wide_cents * (wide_cents - 2.0 * resident_vectors.astype(jnp.float32)), axis=2)
    best = score(rows, pieces, hits)
    both = jnp.stack([best, own])
    one, two, three = (shift(both, "rep", k) for k in (1, 2, 3))
    best_all = jnp.minimum(jnp.minimum(best, two[0]), jnp.minimum(one[0], three[0]))
    own_all = (own + two[1]) + (one[1] + three[1])
    scores = jnp.minimum(best_all, own_all) / math.sqrt(D)
    row_ids = jnp.arange(length)
    rescore = jnp.where(row_ids[None, :] < resident_lengths[:, None], scores, 0.0)
    return (new_postings, new_centroids, rescore)


def solution(mesh):
    return jax.shard_map(
        body,
        mesh=mesh,
        in_specs=(
            P("post", None, "rep"),
            P("post", None),
            P("post"),
            P("post", None),
            P(),
            P("post", None, "rep"),
            P("post", "rep"),
            P("post"),
        ),
        out_specs=(P("post", None, None, "rep"), P("post", None, "rep"), P("post", None)),
        check_vma=False,
    )
```

```python
import functools
import math

import jax
import jax.numpy as jnp
from jax import lax
from jax.experimental import pallas as pl
from jax.experimental.pallas import tpu as pltpu
from jax.sharding import PartitionSpec as P

D = 1024
far_value = 1e30
N_X, N_Z, N_CORE = 4, 8, 2


def centroid_kernel(lengths_hbm, labels_hbm, vectors_hbm, cents_ref, copies_ref,
                    lengths_vec, labels_ref, vectors_ref, sums_ref, half_ref, small_sem, in_sem):
    s_local, length = labels_ref.shape
    group = 8
    n_group = s_local // group

    def fetch(g):
        rows = pl.ds(g * group, group)
        return pltpu.make_async_copy(vectors_hbm.at[rows], vectors_ref.at[rows], in_sem.at[g])

    small = [
        pltpu.make_async_copy(lengths_hbm, lengths_vec.at[0], small_sem.at[0]),
        pltpu.make_async_copy(labels_hbm, labels_ref, small_sem.at[1]),
    ]
    for copy in small:
        copy.start()
    for g in range(n_group):
        fetch(g).start()
    for copy in small:
        copy.wait()

    same = lax.broadcasted_iota(jnp.int32, (s_local, s_local), 0) == lax.broadcasted_iota(
        jnp.int32, (s_local, s_local), 1
    )
    lengths = jnp.sum(
        jnp.where(same, lengths_vec[...].astype(jnp.float32), 0.0), axis=1, keepdims=True
    )
    row_id = lax.broadcasted_iota(jnp.int32, (s_local, length), 1).astype(jnp.float32)
    half_ref[...] = jnp.where(row_id < lengths, labels_ref[...], -100)
    sum_id = lax.broadcasted_iota(jnp.int32, (16, length), 0)
    for g in range(n_group):
        fetch(g).wait()
        total = 0.0
        for j in range(group):
            s = g * group + j
            member = jnp.where(half_ref[s : s + 1, :] + 2 * j == sum_id, 1.0, 0.0)
            total += jnp.dot(
                member.astype(jnp.bfloat16), vectors_ref[s], preferred_element_type=jnp.float32
            )
        sums_ref[g * 2 * group : (g + 1) * 2 * group, :] = total[: 2 * group]

    which = lax.broadcasted_iota(jnp.int32, (2 * s_local, s_local), 0)
    split_id = lax.broadcasted_iota(jnp.int32, (2 * s_local, s_local), 1)
    counts = 0.0
    for h in range(2):
        count = jnp.sum(jnp.where(half_ref[...] == h, 1.0, 0.0), axis=1, keepdims=True)
        pick = jnp.where(which == 2 * split_id + h, 1.0, 0.0).astype(jnp.bfloat16)
        wide = jnp.broadcast_to(count, (s_local, 128)).astype(jnp.bfloat16)
        counts += jnp.dot(pick, wide, preferred_element_type=jnp.float32)
    cents = sums_ref[...] / jnp.concatenate([counts] * (sums_ref.shape[1] // 128), axis=1)
    cents_ref[...] = cents
    rounded = cents.astype(jnp.bfloat16)
    for i in range(copies_ref.shape[0]):
        copies_ref[i] = rounded


def centroids(split_vectors, split_labels, split_lengths):
    s_local, length, dims = split_vectors.shape
    return pl.pallas_call(
        centroid_kernel,
        out_shape=(
            jax.ShapeDtypeStruct((2 * s_local, dims), jnp.float32),
            jax.ShapeDtypeStruct((N_Z, 2 * s_local, dims), jnp.bfloat16),
        ),
        in_specs=[pl.BlockSpec(memory_space=pltpu.HBM)] * 3,
        out_specs=(pl.BlockSpec(memory_space=pltpu.VMEM),) * 2,
        scratch_shapes=[
            pltpu.VMEM((1, s_local), jnp.int32),
            pltpu.VMEM((s_local, length), jnp.int32),
            pltpu.VMEM((s_local, length, dims), jnp.bfloat16),
            pltpu.VMEM((2 * s_local, dims), jnp.float32),
            pltpu.VMEM((s_local, length), jnp.int32),
            pltpu.SemaphoreType.DMA((2,)),
            pltpu.SemaphoreType.DMA((s_local // 8,)),
        ],
        compiler_params=pltpu.CompilerParams(vmem_limit_bytes=56 << 20),
        cost_estimate=pl.CostEstimate(flops=10**8, bytes_accessed=4 << 20, transcendentals=0),
        name="centroids",
    )(split_lengths, split_labels, split_vectors)


def pack_kernel(owners_hbm, lengths_hbm, labels_hbm, vectors_hbm, out_ref,
                owners_ref, lengths_ref, labels_ref, vectors_ref, rank_ref, packed_ref,
                zero_ref, slot_ref, count_ref, out_sem, small_sem, in_sem):
    s_local, length = labels_ref.shape
    half_rows = length // 2
    n_owner = count_ref.shape[0]
    group = 4
    n_group = s_local // group

    def fetch(g):
        rows = pl.ds(g * group, group)
        return pltpu.make_async_copy(vectors_hbm.at[rows], vectors_ref.at[rows], in_sem.at[g])

    small = [
        pltpu.make_async_copy(owners_hbm, owners_ref, small_sem.at[0]),
        pltpu.make_async_copy(lengths_hbm, lengths_ref, small_sem.at[1]),
        pltpu.make_async_copy(labels_hbm, labels_ref, small_sem.at[2]),
    ]
    for copy in small:
        copy.start()
    for g in range(n_group):
        fetch(g).start()
    zero_ref[...] = jnp.zeros_like(zero_ref)
    for o in range(n_owner):
        count_ref[o] = 0
    for copy in small:
        copy.wait()

    @pl.loop(0, s_local // 4)
    def _(g):
        for j in range(4):
            for h in range(2):
                s = g * 4 + j
                owner = owners_ref[h, s]
                slot_ref[2 * s + h] = owner * 2 + count_ref[owner]
                count_ref[owner] = count_ref[owner] + 1

    before = (
        lax.broadcasted_iota(jnp.int32, (length, length), 0)
        < lax.broadcasted_iota(jnp.int32, (length, length), 1)
    )
    labels = labels_ref[...].astype(jnp.float32)
    rank_ref[...] = jnp.dot(
        labels.astype(jnp.bfloat16),
        before.astype(jnp.float32).astype(jnp.bfloat16),
        preferred_element_type=jnp.float32,
    )
    row_id = lax.broadcasted_iota(jnp.int32, (1, length), 1)
    place_id = lax.broadcasted_iota(jnp.int32, (length, length), 0)

    @pl.loop(0, n_group)
    def _(g):
        fetch(g).wait()
        for j in range(group):
            s = g * group + j
            label = labels_ref[pl.ds(s, 1), :]
            rank = rank_ref[pl.ds(s, 1), :].astype(jnp.int32)
            half = jnp.where(row_id < lengths_ref[s], label, 2)
            goes_to = jnp.where(
                half == 0, row_id - rank, jnp.where(half == 1, half_rows + rank, length)
            )
            placement = jnp.where(goes_to == place_id, 1.0, 0.0).astype(jnp.bfloat16)
            placed = jnp.dot(placement, vectors_ref[s], preferred_element_type=jnp.float32)
            packed_ref[2 * s] = placed[:half_rows].astype(jnp.bfloat16)
            packed_ref[2 * s + 1] = placed[half_rows:length].astype(jnp.bfloat16)
            for h in range(2):
                pltpu.make_async_copy(
                    packed_ref.at[2 * s + h], out_ref.at[slot_ref[2 * s + h]], out_sem
                ).start()

        for j in range(n_owner // n_group):
            o = g * (n_owner // n_group) + j
            for k in range(2):
                @pl.when(count_ref[o] <= k)
                def _():
                    pltpu.make_async_copy(zero_ref, out_ref.at[o * 2 + k], out_sem).start()

    pltpu.make_async_copy(out_ref, out_ref, out_sem).wait()


def pack(split_vectors, split_labels, split_lengths, new_owners, n_post):
    s_local, length, dims = split_vectors.shape
    half_rows = length // 2
    return pl.pallas_call(
        pack_kernel,
        out_shape=jax.ShapeDtypeStruct((2 * n_post, half_rows, dims), jnp.bfloat16),
        in_specs=[pl.BlockSpec(memory_space=pltpu.HBM)] * 4,
        out_specs=pl.BlockSpec(memory_space=pltpu.HBM),
        scratch_shapes=[
            pltpu.SMEM((2, s_local), jnp.int32),
            pltpu.SMEM((s_local,), jnp.int32),
            pltpu.VMEM((s_local, length), jnp.int32),
            pltpu.VMEM((s_local, length, dims), jnp.bfloat16),
            pltpu.VMEM((s_local, length), jnp.float32),
            pltpu.VMEM((2 * s_local, half_rows, dims), jnp.bfloat16),
            pltpu.VMEM((half_rows, dims), jnp.bfloat16),
            pltpu.SMEM((2 * s_local,), jnp.int32),
            pltpu.SMEM((n_post,), jnp.int32),
            pltpu.SemaphoreType.DMA,
            pltpu.SemaphoreType.DMA((3,)),
            pltpu.SemaphoreType.DMA((s_local // 4,)),
        ],
        compiler_params=pltpu.CompilerParams(vmem_limit_bytes=56 << 20),
        cost_estimate=pl.CostEstimate(flops=10**9, bytes_accessed=16 << 20, transcendentals=0),
        name="pack",
    )(new_owners.T, split_lengths, split_labels, split_vectors)


def score_kernel(*refs):
    n_rows = len(refs) - N_X * N_CORE - 2
    rows, pieces = refs[:n_rows], refs[n_rows:-2]
    hits_ref, out_ref = refs[-2:]
    n_q = rows[0].shape[0]
    blocks = [jnp.concatenate([p[k] for p in pieces], axis=0) for k in range(n_rows)]
    norm = 0.0
    for block in blocks:
        wide = block.astype(jnp.float32)
        norm += jnp.sum(wide * wide, axis=1, keepdims=True)
    for q in range(n_q):
        cross = 0.0
        for block, ref in zip(blocks, rows):
            cross += lax.dot_general(
                block, ref[q], (((1,), (1,)), ((), ())), preferred_element_type=jnp.float32
            )
        offset = jnp.where(hits_ref[:, q : q + 1] > 0, norm, far_value)
        out_ref[q : q + 1, :] = jnp.min(offset - 2.0 * cross, axis=0, keepdims=True)


def score(rows, pieces, hits):
    n_q, length, dims = rows[0].shape
    return pl.pallas_call(
        score_kernel,
        out_shape=jax.ShapeDtypeStruct((n_q, length), jnp.float32),
        in_specs=[pl.BlockSpec(memory_space=pltpu.VMEM)] * (len(rows) + len(pieces) + 1),
        out_specs=pl.BlockSpec(memory_space=pltpu.VMEM),
        compiler_params=pltpu.CompilerParams(vmem_limit_bytes=40 << 20),
        cost_estimate=pl.CostEstimate(flops=4 * 10**9, bytes_accessed=6 << 20, transcendentals=0),
        name="score",
    )(*rows, *pieces, hits)


def store_kernel(got, out, held, in_sems, out_sems):
    n_copies = in_sems.shape[0]
    step = got.shape[0] // n_copies
    rows = [pl.ds(i * step, step) for i in range(n_copies)]
    reads = [
        pltpu.make_async_copy(got.at[r], held.at[r], in_sems.at[i]) for i, r in enumerate(rows)
    ]
    writes = [
        pltpu.make_async_copy(held.at[r], out.at[r], out_sems.at[i]) for i, r in enumerate(rows)
    ]
    ahead = 2
    for read in reads[:ahead]:
        read.start()
    for i, (read, write) in enumerate(zip(reads, writes)):
        read.wait()
        if i + ahead < n_copies:
            reads[i + ahead].start()
        write.start()
    for write in writes:
        write.wait()


def store(got):
    n_copies = 8
    return pl.pallas_call(
        store_kernel,
        out_shape=jax.ShapeDtypeStruct(got.shape, got.dtype),
        in_specs=[pl.BlockSpec(memory_space=pltpu.HBM)],
        out_specs=pl.BlockSpec(memory_space=pltpu.HBM),
        scratch_shapes=[
            pltpu.VMEM(got.shape, got.dtype),
            pltpu.SemaphoreType.DMA((n_copies,)),
            pltpu.SemaphoreType.DMA((n_copies,)),
        ],
        compiler_params=pltpu.CompilerParams(vmem_limit_bytes=56 << 20),
        cost_estimate=pl.CostEstimate(flops=0, bytes_accessed=12 << 20, transcendentals=0),
        name="store",
    )(got)


def shift(x, axis, k):
    n = lax.axis_size(axis)
    return lax.ppermute(x, axis, [(i, (i + k) % n) for i in range(n)])


def shift_in_plane(x, by_x, by_core):
    pairs = []
    for i in range(N_X * N_Z * N_CORE):
        at_x, at_z, core = i // (N_Z * N_CORE), i // N_CORE % N_Z, i % N_CORE
        to = ((at_x + by_x) % N_X * N_Z + at_z) * N_CORE + (core + by_core) % N_CORE
        pairs.append((i, to))
    return lax.ppermute(x, "post", pairs)


def body(
    split_vectors,
    split_labels,
    split_lengths,
    new_owners,
    neighbour_ids,
    resident_vectors,
    resident_centroids,
    resident_lengths,
):
    n_post, n_rep = lax.axis_size("post"), lax.axis_size("rep")
    s_local, length, dim_share = split_vectors.shape
    res_local = resident_vectors.shape[0]
    new_centroids, copies = centroids(split_vectors, split_labels, split_lengths)

    z_groups = [
        [(x * N_Z + z) * N_CORE + core for z in range(N_Z)]
        for x in range(N_X) for core in range(N_CORE)
    ]
    on_z = lax.all_to_all(
        copies, "post", split_axis=0, concat_axis=0, tiled=True, axis_index_groups=z_groups
    )
    new_centroids, split_vectors = lax.optimization_barrier((new_centroids, split_vectors))
    outgoing = pack(split_vectors, split_labels, split_lengths, new_owners, n_post)
    on_z, outgoing, resident_vectors, resident_centroids, neighbour_ids = lax.optimization_barrier(
        (on_z, outgoing, resident_vectors, resident_centroids, neighbour_ids)
    )
    outgoing = outgoing.reshape(n_post, 2, length // 2, dim_share)
    new_postings = store(
        lax.all_to_all(outgoing, "post", split_axis=0, concat_axis=0, tiled=True)
    )
    new_centroids = new_centroids.reshape(s_local, 2, dim_share)

    rep, post = lax.axis_index("rep"), lax.axis_index("post")
    per_rep = N_Z // n_rep
    parts = [
        lax.dynamic_slice_in_dim(on_z, lax.rem(rep + k, n_rep) * per_rep, per_rep).reshape(
            per_rep * 2 * s_local, dim_share
        )
        for k in range(n_rep)
    ]
    mine = jnp.stack([parts[0]] + [shift(parts[k], "rep", k) for k in range(1, n_rep)])
    pieces = [mine] + [shift_in_plane(mine, k, 0) for k in (1, 3, 2)]
    pieces += [shift_in_plane(piece, 0, 1) for piece in pieces]
    rows = [resident_vectors] + [shift(resident_vectors, "rep", k) for k in range(1, n_rep)]

    my_postings = post * res_local + jnp.arange(res_local)
    ids = []
    for by_core in (0, 1):
        for by_x in (0, 1, 3, 2):
            from_x = lax.rem(post // (N_Z * N_CORE) + N_X - by_x, N_X)
            from_core = lax.rem(post + by_core, N_CORE)
            for z in range(per_rep):
                source = (from_x * N_Z + rep * per_rep + z) * N_CORE + from_core
                ids.append(lax.dynamic_slice_in_dim(neighbour_ids, source * s_local, s_local))
    hits = jnp.any(jnp.concatenate(ids)[:, :, None] == my_postings[None, None, :], axis=1)
    hits = jnp.repeat(hits.astype(jnp.int32), 2, axis=0)
    wide_cents = resident_centroids.astype(jnp.float32)[:, None, :]
    own = jnp.sum(wide_cents * (wide_cents - 2.0 * resident_vectors.astype(jnp.float32)), axis=2)
    best = score(rows, pieces, hits)
    both = jnp.stack([best, own])
    one, two, three = (shift(both, "rep", k) for k in (1, 2, 3))
    best_all = jnp.minimum(jnp.minimum(best, two[0]), jnp.minimum(one[0], three[0]))
    own_all = (own + two[1]) + (one[1] + three[1])
    scores = jnp.minimum(best_all, own_all) / math.sqrt(D)
    row_ids = jnp.arange(length)
    rescore = jnp.where(row_ids[None, :] < resident_lengths[:, None], scores, 0.0)
    return (new_postings, new_centroids, rescore)


def solution(mesh):
    return jax.shard_map(
        body,
        mesh=mesh,
        in_specs=(
            P("post", None, "rep"),
            P("post", None),
            P("post"),
            P("post", None),
            P(),
            P("post", None, "rep"),
            P("post", "rep"),
            P("post"),
        ),
        out_specs=(P("post", None, None, "rep"), P("post", None, "rep"), P("post", None)),
        check_vma=False,
    )
```
